128 devices in a mesh: layer: 2 (over y_hi), row: 8 (over y_lo, x), col: 8 (over z, core).
Axes of the slice: x: 4, y: 4 (y_hi: 2, y_lo: 2; y = y_hi * 2 + y_lo), z: 4, core: 2. Of those that a mesh axis runs over, the one named last changes fastest.
Arguments:
- weights: bfloat16 [16, 8192, 8192], P('layer', 'row', 'col'), may hold values from -6 to 6
- col_factor: bfloat16 [8192, 256], P('col'), may hold values from -0.0625 to 0.0625
- layer_factor: float32 [16, 4], P('layer'), may hold values from -1.5 to 1.5
- row_factor: float32 [8192, 256], P('row'), may hold values from -0.0625 to 0.0625
Outputs:
- row_update: float32 [8192, 256], P('row')
- core_out: float32 [256, 1024], replicated
The draws below stay inside these ranges and needn't reach their ends.
All inputs are finite; a program needn't handle non-finite values.
Results may differ from the reference program's by a relative error of at most 0.0003.
Values sent between devices are 32-bit elements; how exact they have to be, the bound alone decides.
No kernel may reach another device: no remote copies, remote signals or barrier semaphores. Data moves between devices by JAX's collectives and lax.ppermute only.
A program may use at most 128 MiB of HBM per device.

```python
import jax
import jax.numpy as jnp
from jax import lax

R = 8192
C = 8192
RC = 256
RL = 4
RR = 256
L = 16


def steps_of(stream_key, extent, cuts, smallest, top_value):
    level = 1.0
    for dim, blocks in cuts:
        steps = jax.random.uniform(jax.random.fold_in(jax.random.fold_in(stream_key, 6), dim), (blocks,), jnp.float32, smallest / len(cuts), top_value / len(cuts))
        level = level * jnp.repeat(jnp.exp(steps), extent[dim] // blocks).reshape((-1,) + (1,) * (len(extent) - 1 - dim))
    return level


def gaussian(stream_key, dims, deviation, reach, cuts=(), kind=jnp.bfloat16):
    factor_of = steps_of(stream_key, dims, cuts, -0.22, 0.18) if cuts else 1.0
    values = jax.random.normal(stream_key, dims, jnp.float32) * deviation * factor_of
    return jnp.minimum(jnp.maximum(values, -reach), reach).astype(kind)


def setup_inputs(seed: int = 0) -> dict:
    key_of = jax.random.split(jax.random.key(seed), 5)
    return {
        "weights": gaussian(key_of[0], (L, R, C), 1.0, 6.0, ((0, 2), (1, 8), (2, 8))),
        "col_factor": gaussian(key_of[1], (C, RC), C ** -0.5, 0.0625, ((0, 8),)),
        "layer_factor": gaussian(key_of[2], (L, RL), L ** -0.5, 1.5, ((0, 2),), jnp.float32),
        "row_factor": gaussian(key_of[3], (R, RR), R ** -0.5, 0.0625, ((0, 8),), jnp.float32),
    }


highest = lax.Precision.HIGHEST

def reference(weights, col_factor, layer_factor, row_factor):

    def per_layer(layer_block):
        return jnp.dot(layer_block, col_factor, preferred_element_type=jnp.float32)
    projected = lax.map(per_layer, weights)
    contracted = jnp.einsum('lrk,lm->rmk', projected, layer_factor.astype(jnp.float32), precision=highest)
    unfolded = contracted.reshape(R, RL * RC)
    cross = jnp.dot(unfolded.T, row_factor, precision=highest, preferred_element_type=jnp.float32)
    row_update = jnp.dot(unfolded, cross, precision=highest, preferred_element_type=jnp.float32) / jnp.sqrt(jnp.float32(RL * RC))
    core_out = jnp.dot(row_update.T, unfolded, precision=highest, preferred_element_type=jnp.float32) / jnp.sqrt(jnp.float32(R))
    return (row_update, core_out)
```

```python
import jax
import jax.numpy as jnp
from jax import lax
from jax.experimental import pallas as pl
from jax.experimental.pallas import tpu as pltpu
from jax.sharding import Mesh, PartitionSpec as P

R = 8192
RC = 256
RL = 4

AXES = ("yhi", "ylo", "x", "z", "core")
CHIPS = AXES[:4]
TILE = 128
HALF = RL * RC // 2
f32 = jnp.float32
bf16 = jnp.bfloat16


def parts_of(v):
    hi = v.astype(bf16)
    return hi, (v - hi.astype(f32)).astype(bf16)


def dot3(a, b, dims):
    ah, al = parts_of(a)
    bh, bl = parts_of(b)

    def dot(p, q):
        return lax.dot_general(p, q, (dims, ((), ())), preferred_element_type=f32)

    return dot(ah, bh) + (dot(ah, bl) + dot(al, bh))


def to_tiles(ref, value):
    cols = value.shape[1] // 128
    for a in range(value.shape[0] // 8):
        for b in range(cols):
            ref[a * cols + b] = value[8 * a : 8 * a + 8, 128 * b : 128 * b + 128]


def contract_kernel(order, lf, w, c, send, keep, d):
    layers = w.shape[0]
    for l in range(layers):
        d[l] = jnp.dot(w[l], c[...], preferred_element_type=f32)
    for half, out in ((0, send), (1, keep)):
        for j in range(RL // 2):
            m = half * (RL // 2) + j
            acc = d[0] * lf[0, m]
            for l in range(1, layers):
                acc = acc + d[l] * lf[l, m]
            out[:, j * RC : (j + 1) * RC] = acc


def contract(order, lf, w, c, first, count):
    layers, _, cols = w.shape
    out = jax.ShapeDtypeStruct((count * TILE, HALF), f32)
    spec = pl.BlockSpec((TILE, HALF), lambda i, order: (i, 0))
    return pl.pallas_call(
        contract_kernel,
        out_shape=(out, out),
        grid_spec=pltpu.PrefetchScalarGridSpec(
            num_scalar_prefetch=1,
            grid=(count,),
            in_specs=[
                pl.BlockSpec(memory_space=pltpu.SMEM),
                pl.BlockSpec((layers, TILE, cols), lambda i, order: (0, order[first + i], 0)),
                pl.BlockSpec((cols, RC), lambda i, order: (0, 0)),
            ],
            out_specs=(spec, spec),
            scratch_shapes=[pltpu.VMEM((layers, TILE, RC), f32)],
        ),
        cost_estimate=pl.CostEstimate(
            flops=2 * layers * count * TILE * cols * RC,
            bytes_accessed=2 * layers * count * TILE * cols + 8 * count * TILE * HALF,
            transcendentals=0,
        ),
        name="contract",
    )(order, lf, w, c)


def cross_kernel(first, order, keep, recv, rf, *refs):
    prior = refs[0] if len(refs) == 4 else None
    va, vb, ct = refs[-3:]
    rows = [rf[pl.ds(pl.multiple_of(order[first + i] * TILE, TILE), TILE), :] for i in range(4)]
    total = None
    for out, at in ((va, 0), (vb, 1)):
        v = keep[at * 256 : at * 256 + 256] + recv[at * 256 : at * 256 + 256]
        out[...] = v
        f = jnp.concatenate(rows[2 * at : 2 * at + 2], axis=0)
        term = dot3(f, v, ((0,), (0,)))
        total = term if total is None else total + term
    cols = HALF // 128
    for a in range(RC // 8):
        for b in range(cols):
            t = total[8 * a : 8 * a + 8, 128 * b : 128 * b + 128]
            if prior is not None:
                t = t + prior[a * cols + b]
            ct[a * cols + b] = t


def cross_part(order, keep, recv, rf, first, prior):
    vmem = pl.BlockSpec(memory_space=pltpu.VMEM)
    ops = [keep, recv, rf] + ([] if prior is None else [prior])
    v = jax.ShapeDtypeStruct((256, HALF), f32)
    ct = jax.ShapeDtypeStruct((RC * HALF // 1024, 8, 128), f32)

    def kernel(*refs):
        cross_kernel(first, *refs)

    return pl.pallas_call(
        kernel,
        out_shape=(v, v, ct),
        in_specs=[pl.BlockSpec(memory_space=pltpu.SMEM)] + [vmem] * len(ops),
        out_specs=(vmem, vmem, vmem),
        cost_estimate=pl.CostEstimate(
            flops=6 * 512 * RC * HALF, bytes_accessed=8 << 20, transcendentals=0
        ),
        name="cross_part",
    )(order, *ops)


def rows_kernel(ct, ka, kb, zp, u, full):
    cols = HALF // 128
    for a in range(RC // 8):
        for b in range(cols):
            full[8 * a : 8 * a + 8, 128 * b : 128 * b + 128] = ct[a * cols + b]
    v = ka[...] + kb[...]
    u[...] = v
    zp[...] = dot3(v, full[...], ((1,), (1,)))


def core_kernel(zp, zr, u, z, ct):
    width_scale = 1.0 / jnp.sqrt(f32(RL * RC))
    row_scale = 1.0 / jnp.sqrt(f32(R))
    rows = (zp[...] + zr[...]) * width_scale
    z[...] = rows
    to_tiles(ct, dot3(rows, u[...], ((0,), (0,))) * row_scale)


def finish_kernel(core, mine, other, out):
    cols = HALF // 128
    for ref, at in ((mine, core[0]), (other, 1 - core[0])):
        base = at * HALF
        for b in range(cols):
            lane = pl.ds(pl.multiple_of(base + 128 * b, 128), 128)
            for a in range(RC // 8):
                out[8 * a : 8 * a + 8, lane] = ref[a * cols + b]


def whole(kernel, outs, n_in, scratch=(), smem=0, name=None):
    vmem = pl.BlockSpec(memory_space=pltpu.VMEM)
    return pl.pallas_call(
        kernel,
        out_shape=outs,
        in_specs=[pl.BlockSpec(memory_space=pltpu.SMEM)] * smem + [vmem] * n_in,
        out_specs=jax.tree.map(lambda _: vmem, outs),
        scratch_shapes=list(scratch),
        name=name,
    )


def shift(v, axis, size, by):
    return lax.ppermute(v, axis, [(i, (i + by) % size) for i in range(size)])


def sum_over_chips(tiles):
    n = lax.axis_size(CHIPS)
    v = tiles.reshape(n, -1, 128)
    v = lax.all_to_all(v, CHIPS, 0, 0, tiled=True)
    s = jnp.sum(v, axis=0)
    g = lax.all_to_all(jnp.broadcast_to(s, v.shape), CHIPS, 0, 0, tiled=True)
    return g.reshape(tiles.shape)


def body(weights, col_factor, layer_factor, row_factor):
    yhi, z, core = lax.axis_index("yhi"), lax.axis_index("z"), lax.axis_index("core")
    away = jnp.array([2, 2, 1, 1, 3, 3, 0, 0], jnp.int32)
    flip = jnp.array([1, 0] * 4, jnp.int32)
    order = ((z + away) % 4) * 2 + (yhi ^ flip)
    swapped = jnp.concatenate([layer_factor[:, RL // 2 :], layer_factor[:, : RL // 2]], axis=1)
    lf = jnp.where(core == 0, swapped, layer_factor)

    send1, keep1 = contract(order, lf, weights, col_factor, 0, 4)
    recv1 = shift(send1, "core", 2, 1)
    send2, keep2 = contract(order, lf, weights, col_factor, 4, 4)
    recv2 = shift(send2, "core", 2, 1)
    v2, v1, ct1 = cross_part(order, keep1, recv1, row_factor, 0, None)
    v3, v0, ct = cross_part(order, keep2, recv2, row_factor, 4, ct1)

    r2 = shift(v2, "z", 4, 2)
    r1 = shift(v1, "z", 4, 1)
    r3 = shift(v3, "z", 4, 3)
    cross = sum_over_chips(ct)
    block = v0 + r1 + r2 + r3
    ka = block[TILE:]
    kb = shift(block[:TILE], "yhi", 2, 1)

    out = jax.ShapeDtypeStruct
    zp, u = whole(
        rows_kernel,
        (out((TILE, RC), f32), out((TILE, HALF), f32)),
        3,
        [pltpu.VMEM((RC, HALF), f32)],
        name="rows_part",
    )(cross, ka, kb)
    zr = shift(zp, "core", 2, 1)
    zrows, ct = whole(
        core_kernel, (out((TILE, RC), f32), out(ct.shape, f32)), 3, name="core_part"
    )(zp, zr, u)

    mine = sum_over_chips(ct)
    other = shift(mine, "core", 2, 1)
    core_out = whole(
        finish_kernel, out((RC, 2 * HALF), f32), 2, smem=1, name="finish_core"
    )(core[None], mine, other)

    n = lax.axis_size(("z", "yhi"))
    part = lax.dynamic_slice_in_dim(zrows, core * (TILE // 2), TILE // 2, 0)
    got = lax.all_to_all(
        jnp.broadcast_to(part, (n,) + part.shape), ("z", "yhi"), 0, 0, tiled=True
    )
    more = shift(got, "core", 2, 1)
    pair = jnp.where(core == 0, jnp.stack([got, more], 1), jnp.stack([more, got], 1))
    return pair.reshape(n * TILE, RC), core_out


def solution(mesh):
    fine = Mesh(mesh.devices.reshape(2, 2, 4, 4, 2), AXES)
    return jax.shard_map(
        body,
        mesh=fine,
        in_specs=(
            P("yhi", ("ylo", "x"), ("z", "core")),
            P(("z", "core"), None),
            P("yhi", None),
            P(("ylo", "x"), None),
        ),
        out_specs=(P(("ylo", "x"), None), P()),
        check_vma=False,
    )
```

```python
import functools

import jax
import jax.numpy as jnp
from jax import lax
from jax.experimental import pallas as pl
from jax.experimental.pallas import tpu as pltpu
from jax.sharding import Mesh, PartitionSpec as P


R = 8192
RC = 256
RL = 4

AXES = ("yhi", "ylo", "x", "z", "core")
PLANE = AXES[:3]
CHIPS = AXES[:4]
SUB = 64
BLOCK = 256
HALF = RL * RC // 2
COLS = HALF // 128
f32 = jnp.float32
bf16 = jnp.bfloat16
SMEM = pl.BlockSpec(memory_space=pltpu.SMEM)
VMEM = pl.BlockSpec(memory_space=pltpu.VMEM)
MIB = 1 << 20


def parts_of(v):
    hi = v.astype(bf16)
    return hi, (v - hi.astype(f32)).astype(bf16)


def dot3(a, b, dims):
    ah, al = parts_of(a)
    bh, bl = parts_of(b)

    def dot(p, q):
        return lax.dot_general(p, q, (dims, ((), ())), preferred_element_type=f32)

    return dot(ah, bh) + (dot(ah, bl) + dot(al, bh))


def call(kernel, outs, ops, smem=0, scratch=(), vmem=16, cost=None):
    return pl.pallas_call(
        kernel,
        out_shape=outs,
        in_specs=[SMEM] * smem + [VMEM] * (len(ops) - smem),
        out_specs=jax.tree.map(lambda _: VMEM, outs),
        scratch_shapes=list(scratch),
        compiler_params=pltpu.CompilerParams(vmem_limit_bytes=vmem * MIB),
        cost_estimate=cost,
    )(*ops)


def shape(*dims):
    return jax.ShapeDtypeStruct(dims, f32)


def half_block(i, where):
    k = i // 2
    away = jnp.where(k == 0, 2, jnp.where(k == 1, 1, jnp.where(k == 2, 3, 0)))
    flip = 1 - i % 2
    return ((where[0] + away) % 4) * 2 + (where[1] + flip) % 2


def contract_kernel(where, lf, w_a, w_b, c, send, keep, d):
    layers, rows, cols = w_a.shape
    per = rows // SUB
    for s in range(2 * per):
        w = (w_a, w_b)[s // per]
        at = (s % per) * SUB
        part = w[:, at : at + SUB, :].reshape(layers * SUB, cols)
        d[s] = jnp.dot(part, c[...], preferred_element_type=f32).reshape(layers, SUB, RC)
    theirs = (1 - where[2]) * (RL // 2)
    step = 16
    for s in range(2 * per):
        for r in range(0, SUB, step):
            v = [d[s, l, r : r + step, :] for l in range(layers)]
            for base, out in ((theirs, send), (RL // 2 - theirs, keep)):
                for j in range(RL // 2):
                    acc = v[0] * lf[base + j, 0]
                    for l in range(1, layers):
                        acc = acc + v[l] * lf[base + j, l]
                    out[s * SUB + r : s * SUB + r + step, j * RC : (j + 1) * RC] = acc


def contract(where, lf, w, c, first, count):
    layers, _, cols = w.shape
    out = shape(count * BLOCK, HALF)
    spec = pl.BlockSpec((BLOCK, HALF), lambda i, where: (i, 0))

    def half(n):
        return pl.BlockSpec(
            (layers, BLOCK // 2, cols),
            lambda i, where: (0, half_block(2 * (first + i) + n, where), 0),
        )

    return pl.pallas_call(
        contract_kernel,
        out_shape=(out, out),
        grid_spec=pltpu.PrefetchScalarGridSpec(
            num_scalar_prefetch=1,
            grid=(count,),
            in_specs=[SMEM, half(0), half(1), pl.BlockSpec((cols, RC), lambda i, where: (0, 0))],
            out_specs=(spec, spec),
            scratch_shapes=[pltpu.VMEM((BLOCK // SUB, layers, SUB, RC), f32)],
        ),
        compiler_params=pltpu.CompilerParams(vmem_limit_bytes=50 * MIB),
        cost_estimate=pl.CostEstimate(
            flops=2 * layers * count * BLOCK * cols * RC,
            bytes_accessed=2 * layers * count * BLOCK * cols + 8 * count * BLOCK * HALF,
            transcendentals=0,
        ),
        name="contract",
    )(where, lf, w, w, c)


def cross_kernel(first, count, where, keep, recv, rf, *refs):
    prior = refs[0] if len(refs) > count + 1 else None
    blocks, ct = refs[-count - 1 : -1], refs[-1]
    half = BLOCK // 2
    total = None
    for n, out in enumerate(blocks):
        v = keep[n * BLOCK : (n + 1) * BLOCK] + recv[n * BLOCK : (n + 1) * BLOCK]
        out[...] = v
        f = jnp.concatenate(
            [
                rf[pl.ds(pl.multiple_of(half_block(2 * (first + n) + h, where) * half, half), half), :]
                for h in range(2)
            ],
            axis=0,
        )
        term = dot3(f, v, ((0,), (0,)))
        total = term if total is None else total + term
    for a in range(RC // 8):
        for b in range(COLS):
            t = total[8 * a : 8 * a + 8, 128 * b : 128 * b + 128]
            if prior is not None:
                t = t + prior[a * COLS + b]
            ct[a * COLS + b] = t


def cross_part(where, keep, recv, rf, first, count, prior):
    ops = [where, keep, recv, rf] + ([] if prior is None else [prior])
    return call(
        functools.partial(cross_kernel, first, count),
        [shape(BLOCK, HALF)] * count + [shape(RC * HALF // 1024, 8, 128)],
        ops,
        smem=1,
        vmem=20,
        cost=pl.CostEstimate(
            flops=6 * count * BLOCK * RC * HALF, bytes_accessed=4 * MIB, transcendentals=0
        ),
    )


def rows_kernel(ct, ka, kb, zp, u, full):
    for a in range(RC // 8):
        for b in range(COLS):
            full[8 * a : 8 * a + 8, 128 * b : 128 * b + 128] = ct[a * COLS + b]
    v = ka[...] + kb[...]
    u[...] = v
    zp[...] = dot3(v, full[...], ((1,), (1,)))


def core_kernel(where, zp, zr, u, z, ct):
    width_scale = 1.0 / jnp.sqrt(f32(RL * RC))
    row_scale = 1.0 / jnp.sqrt(f32(R))
    rows = (zp[...] + zr[...]) * width_scale
    half = rows.shape[0] // 2
    mine = pl.ds(pl.multiple_of(where[2] * half, half), half)
    z[...] = (zp[mine] + zr[mine]) * width_scale
    core = dot3(rows, u[...], ((0,), (0,))) * row_scale
    for a in range(RC // 8):
        for b in range(COLS):
            ct[a * COLS + b] = core[8 * a : 8 * a + 8, 128 * b : 128 * b + 128]


def finish_core_kernel(where, mine, other, out):
    for ref, at in ((mine, where[2]), (other, 1 - where[2])):
        for b in range(COLS):
            lane = pl.ds(pl.multiple_of(at * HALF + 128 * b, 128), 128)
            for a in range(RC // 8):
                out[8 * a : 8 * a + 8, lane] = ref[a * COLS + b]


def finish_rows_kernel(where, mine, other, out):
    quarter = BLOCK // 4
    for ref, at in ((mine, where[2]), (other, 1 - where[2])):
        for k in range(4):
            base = ((where[0] + 4 - k) % 4) * BLOCK + at * quarter
            for n in range(2):
                row = base + (where[1] + n) % 2 * (BLOCK // 2)
                rows = pl.ds(pl.multiple_of(row, quarter), quarter)
                i = (2 * k + n) * quarter
                out[rows, :] = ref[i : i + quarter, :]


def block_kernel(v0, r2, r1, r3, away, keep):
    half = BLOCK // 2
    for out, at in ((away, 0), (keep, half)):
        at = pl.ds(at, half)
        out[...] = (v0[at] + r2[at]) + (r1[at] + r3[at])


def gathered_kernel(v, out):
    total = v[0]
    for i in range(1, v.shape[0]):
        total = total + v[i]
    out[...] = total


def spread_kernel(*refs):
    out = refs[-1]
    if len(refs) == 2:
        v = refs[0][0]
        for i in range(1, out.shape[0]):
            v = v + refs[0][i]
    else:
        s, s1, s2, s3 = (ref[...] for ref in refs[:-1])
        v = (s + s2) + (s1 + s3)
    for i in range(out.shape[0]):
        out[i] = v


def join_kernel(*refs):
    out = refs[-1]
    rows = refs[0].shape[0]
    for i, ref in enumerate(refs[:-1]):
        out[i * rows : (i + 1) * rows] = ref[...]


def shift(v, axis, size, by):
    return lax.ppermute(v, axis, [(i, (i + by) % size) for i in range(size)])


def exchange(v, axes):
    return lax.all_to_all(v, axes, 0, 0, tiled=True)


def sum_over_planes(tiles):
    n = lax.axis_size(PLANE)
    v = exchange(tiles.reshape(n, -1, 128), PLANE)
    s = call(gathered_kernel, shape(*v.shape[1:]), [v])
    s1, s2, s3 = (shift(s, "z", 4, k) for k in (1, 2, 3))
    b = call(spread_kernel, shape(*v.shape), [s, s1, s2, s3])
    return exchange(b, PLANE).reshape(tiles.shape)


def sum_over_chips(tiles):
    n = lax.axis_size(CHIPS)
    v = exchange(tiles.reshape(n, -1, 128), CHIPS)
    b = call(spread_kernel, shape(*v.shape), [v])
    return exchange(b, CHIPS).reshape(tiles.shape)


def body(weights, col_factor, layer_factor, row_factor):
    weights, col_factor = (pltpu.with_memory_space_constraint(v, pltpu.HBM) for v in (weights, col_factor))
    where = jnp.stack([lax.axis_index(a) for a in ("z", "yhi", "core")])
    lf = pltpu.with_memory_space_constraint(layer_factor.T, pltpu.HBM)

    send1, keep1 = contract(where, lf, weights, col_factor, 0, 3)
    recv1 = shift(send1, "core", 2, 1)
    send2, keep2 = contract(where, lf, weights, col_factor, 3, 1)
    recv2 = shift(send2, "core", 2, 1)
    v2, v1, v3, ct = cross_part(where, keep1, recv1, row_factor, 0, 3, None)
    r2 = shift(v2, "z", 4, 2)
    r1 = shift(v1, "z", 4, 1)
    r3 = shift(v3, "z", 4, 3)
    v0, ct = cross_part(where, keep2, recv2, row_factor, 3, 1, ct)
    cross = sum_over_planes(ct)

    rows = BLOCK // 2
    away, ka = call(block_kernel, [shape(rows, HALF)] * 2, [v0, r2, r1, r3])
    kb = shift(away, "yhi", 2, 1)

    zp, u = call(
        rows_kernel,
        [shape(rows, RC), shape(rows, HALF)],
        [cross, ka, kb],
        scratch=[pltpu.VMEM((RC, HALF), f32)],
    )
    zr = shift(zp, "core", 2, 1)
    z, ct = call(core_kernel, [shape(rows // 2, RC), shape(*ct.shape)], [where, zp, zr, u], smem=1)

    zy = shift(z, "yhi", 2, 1)
    both = call(join_kernel, shape(rows, RC), [z, zy])
    gathered = [both] + [shift(both, "z", 4, k) for k in (1, 2, 3)]
    four = call(join_kernel, shape(4 * rows, RC), gathered)
    other = shift(four, "core", 2, 1)
    row_update = call(finish_rows_kernel, shape(8 * rows, RC), [where, four, other], smem=1)

    mine = sum_over_chips(ct)
    other = shift(mine, "core", 2, 1)
    core_out = call(finish_core_kernel, shape(RC, 2 * HALF), [where, mine, other], smem=1)
    return row_update, core_out


def solution(mesh):
    fine = Mesh(mesh.devices.reshape(2, 2, 4, 4, 2), AXES)
    return jax.shard_map(
        body,
        mesh=fine,
        in_specs=(
            P("yhi", ("ylo", "x"), ("z", "core")),
            P(("z", "core"), None),
            P("yhi", None),
            P(("ylo", "x"), None),
        ),
        out_specs=(P(("ylo", "x"), None), P()),
        check_vma=False,
    )
```

```python
import functools

import jax
import jax.numpy as jnp
from jax import lax
from jax.experimental import pallas as pl
from jax.experimental.pallas import tpu as pltpu
from jax.sharding import Mesh, PartitionSpec as P


R = 8192
RC = 256
RL = 4

AXES = ("yhi", "ylo", "x", "z", "core")
PLANE = AXES[:3]
CHIPS = AXES[:4]
SUB = 64
BLOCK = 256
HALF = RL * RC // 2
COLS = HALF // 128
f32 = jnp.float32
bf16 = jnp.bfloat16
SMEM = pl.BlockSpec(memory_space=pltpu.SMEM)
VMEM = pl.BlockSpec(memory_space=pltpu.VMEM)
MIB = 1 << 20


def parts_of(v):
    hi = v.astype(bf16)
    return hi, (v - hi.astype(f32)).astype(bf16)


def dot3(a, b, dims):
    ah, al = parts_of(a)
    bh, bl = parts_of(b)

    def dot(p, q):
        return lax.dot_general(p, q, (dims, ((), ())), preferred_element_type=f32)

    return dot(ah, bh) + (dot(ah, bl) + dot(al, bh))


def call(kernel, outs, ops, smem=0, scratch=(), vmem=16, cost=None):
    return pl.pallas_call(
        kernel,
        out_shape=outs,
        in_specs=[SMEM] * smem + [VMEM] * (len(ops) - smem),
        out_specs=jax.tree.map(lambda _: VMEM, outs),
        scratch_shapes=list(scratch),
        compiler_params=pltpu.CompilerParams(vmem_limit_bytes=vmem * MIB),
        cost_estimate=cost,
    )(*ops)


def shape(*dims):
    return jax.ShapeDtypeStruct(dims, f32)


def half_block(i):
    away = (2, 1, 3, 0)[i // 2]
    return ((lax.axis_index("z") + away) % 4) * 2 + (lax.axis_index("yhi") + 1 - i % 2) % 2


def mix_columns(lf, d, subs, send, keep):
    layers = d.shape[1]
    theirs = (1 - lax.axis_index("core")) * (RL // 2)
    step = 16
    for s in subs:
        for r in range(0, SUB, step):
            v = [d[s, l, r : r + step, :] for l in range(layers)]
            for base, out in ((theirs, send), (RL // 2 - theirs, keep)):
                for j in range(RL // 2):
                    acc = v[0] * lf[base + j, 0]
                    for l in range(1, layers):
                        acc = acc + v[l] * lf[base + j, l]
                    out[s * SUB + r : s * SUB + r + step, j * RC : (j + 1) * RC] = acc


def contract_kernel(lf, w, c, send, keep, ahead, c_copy, wbuf, d, sems):
    layers, _, cols = w.shape
    count, last = wbuf.shape[0], ahead.shape[0]
    per = BLOCK // 2 // SUB

    def copy(s):
        row = half_block(s // per) * (BLOCK // 2) + s % per * SUB
        rows = pl.ds(pl.multiple_of(row, SUB), SUB)
        target = wbuf.at[s] if s < count else ahead.at[s - count]
        return pltpu.make_async_copy(w.at[:, rows, :], target, sems.at[s])

    fetch = pltpu.make_async_copy(c, c_copy, sems.at[count + last])
    fetch.start()
    for s in range(count + last):
        copy(s).start()
    fetch.wait()
    at = 0
    for size in (1, 3) + (4,) * (count // 4 - 1):
        subs = range(at, at + size)
        for s in subs:
            copy(s).wait()
        for s in subs:
            part = wbuf[s].reshape(layers * SUB, cols)
            d[s] = jnp.dot(part, c_copy[...], preferred_element_type=f32).reshape(layers, SUB, RC)
        mix_columns(lf, d, subs, send, keep)
        at += size
    for s in range(count, count + last):
        copy(s).wait()


def contract(lf, w, c):
    layers, rows, cols = w.shape
    count = (rows - BLOCK) // SUB
    last = BLOCK // SUB
    out = shape(rows - BLOCK, HALF)
    hbm = pl.BlockSpec(memory_space=pl.ANY)
    return pl.pallas_call(
        contract_kernel,
        out_shape=(
            out,
            out,
            jax.ShapeDtypeStruct((last, layers, SUB, cols), bf16),
            jax.ShapeDtypeStruct(c.shape, bf16),
        ),
        in_specs=[SMEM, hbm, hbm],
        out_specs=(VMEM,) * 4,
        scratch_shapes=[
            pltpu.VMEM((count, layers, SUB, cols), bf16),
            pltpu.VMEM((count, layers, SUB, RC), f32),
            pltpu.SemaphoreType.DMA((count + last + 1,)),
        ],
        compiler_params=pltpu.CompilerParams(vmem_limit_bytes=40 * MIB),
        cost_estimate=pl.CostEstimate(
            flops=2 * layers * (rows - BLOCK) * cols * RC,
            bytes_accessed=2 * layers * rows * cols,
            transcendentals=0,
        ),
        name="contract",
    )(lf, w, c)


def contract_last_kernel(lf, w, c, send, keep, d):
    last, layers, _, cols = w.shape
    for s in range(last):
        part = w[s].reshape(layers * SUB, cols)
        d[s] = jnp.dot(part, c[...], preferred_element_type=f32).reshape(layers, SUB, RC)
    mix_columns(lf, d, range(last), send, keep)


def contract_last(lf, w, c):
    last, layers, _, cols = w.shape
    return call(
        contract_last_kernel,
        [shape(BLOCK, HALF)] * 2,
        [lf, w, c],
        smem=1,
        scratch=[pltpu.VMEM((last, layers, SUB, RC), f32)],
        cost=pl.CostEstimate(
            flops=2 * layers * BLOCK * cols * RC, bytes_accessed=MIB, transcendentals=0
        ),
    )


def cross_kernel(first, count, keep, recv, rf, *refs):
    prior = refs[0] if len(refs) > 2 * count + 1 else None
    blocks, ct = refs[-2 * count - 1 : -1], refs[-1]
    half = BLOCK // 2
    total = None
    for n in range(count):
        v = keep[n * BLOCK : (n + 1) * BLOCK] + recv[n * BLOCK : (n + 1) * BLOCK]
        blocks[2 * n][...] = v[:half]
        blocks[2 * n + 1][...] = v[half:]
        f = jnp.concatenate(
            [
                rf[pl.ds(pl.multiple_of(half_block(2 * (first + n) + h) * half, half), half), :]
                for h in range(2)
            ],
            axis=0,
        )
        term = dot3(f, v, ((0,), (0,)))
        total = term if total is None else total + term
    for a in range(RC // 8):
        for b in range(COLS):
            t = total[8 * a : 8 * a + 8, 128 * b : 128 * b + 128]
            if prior is not None:
                t = t + prior[a * COLS + b]
            ct[a * COLS + b] = t


def cross_part(keep, recv, rf, first, count, prior):
    ops = [keep, recv, rf] + ([] if prior is None else [prior])
    return call(
        functools.partial(cross_kernel, first, count),
        [shape(BLOCK // 2, HALF)] * (2 * count) + [shape(RC * HALF // 1024, 8, 128)],
        ops,
        vmem=20,
        cost=pl.CostEstimate(
            flops=6 * count * BLOCK * RC * HALF, bytes_accessed=4 * MIB, transcendentals=0
        ),
    )


def rows_kernel(ct, ka, kb, zp, u, full):
    for a in range(RC // 8):
        for b in range(COLS):
            full[8 * a : 8 * a + 8, 128 * b : 128 * b + 128] = ct[a * COLS + b]
    v = ka[...] + kb[...]
    u[...] = v
    zp[...] = dot3(v, full[...], ((1,), (1,)))


def core_kernel(zp, zr, u, z, ct):
    width_scale = 1.0 / jnp.sqrt(f32(RL * RC))
    row_scale = 1.0 / jnp.sqrt(f32(R))
    rows = (zp[...] + zr[...]) * width_scale
    half = rows.shape[0] // 2
    mine = pl.ds(pl.multiple_of(lax.axis_index("core") * half, half), half)
    z[...] = (zp[mine] + zr[mine]) * width_scale
    core = dot3(rows, u[...], ((0,), (0,))) * row_scale
    for a in range(RC // 8):
        for b in range(COLS):
            ct[a * COLS + b] = core[8 * a : 8 * a + 8, 128 * b : 128 * b + 128]


def finish_core_kernel(mine, other, out):
    core = lax.axis_index("core")
    for ref, at in ((mine, core), (other, 1 - core)):
        for b in range(COLS):
            lane = pl.ds(pl.multiple_of(at * HALF + 128 * b, 128), 128)
            for a in range(RC // 8):
                out[8 * a : 8 * a + 8, lane] = ref[a * COLS + b]


def finish_rows_kernel(mine, other, out):
    z, yhi, core = (lax.axis_index(a) for a in ("z", "yhi", "core"))
    quarter = BLOCK // 4
    for ref, at in ((mine, core), (other, 1 - core)):
        for k in range(4):
            base = ((z + 4 - k) % 4) * BLOCK + at * quarter
            for n in range(2):
                row = base + (yhi + n) % 2 * (BLOCK // 2)
                rows = pl.ds(pl.multiple_of(row, quarter), quarter)
                i = (2 * k + n) * quarter
                out[rows, :] = ref[i : i + quarter, :]


def relay_kernel(a, b, c, d, ab, cd):
    ab[...] = a[...] + b[...]
    cd[...] = c[...] + d[...]


def block_kernel(a0, a1, a2, b0, b1, b2, away, keep):
    away[...] = (a0[...] + a1[...]) + a2[...]
    keep[...] = (b0[...] + b1[...]) + b2[...]


def gathered_kernel(v, out):
    total = v[0]
    for i in range(1, v.shape[0]):
        total = total + v[i]
    out[...] = total


def spread_kernel(*refs):
    out = refs[-1]
    if len(refs) == 2:
        v = refs[0][0]
        for i in range(1, out.shape[0]):
            v = v + refs[0][i]
    else:
        s, s1, s2, s3 = (ref[...] for ref in refs[:-1])
        v = (s + s2) + (s1 + s3)
    for i in range(out.shape[0]):
        out[i] = v


def join_kernel(*refs):
    out = refs[-1]
    rows = refs[0].shape[0]
    for i, ref in enumerate(refs[:-1]):
        out[i * rows : (i + 1) * rows] = ref[...]


def shift(v, axis, size, by):
    return lax.ppermute(v, axis, [(i, (i + by) % size) for i in range(size)])


def exchange(v, axes):
    return lax.all_to_all(v, axes, 0, 0, tiled=True)


def sum_over_planes(tiles):
    n = lax.axis_size(PLANE)
    v = exchange(tiles.reshape(n, -1, 128), PLANE)
    s = call(gathered_kernel, shape(*v.shape[1:]), [v])
    s1, s2, s3 = (shift(s, "z", 4, k) for k in (1, 2, 3))
    b = call(spread_kernel, shape(*v.shape), [s, s1, s2, s3])
    return exchange(b, PLANE).reshape(tiles.shape)


def sum_over_chips(tiles):
    n = lax.axis_size(CHIPS)
    v = exchange(tiles.reshape(n, -1, 128), CHIPS)
    b = call(spread_kernel, shape(*v.shape), [v])
    return exchange(b, CHIPS).reshape(tiles.shape)


def body(weights, col_factor, layer_factor, row_factor):
    weights, col_factor = (pltpu.with_memory_space_constraint(v, pltpu.HBM) for v in (weights, col_factor))
    lf = pltpu.with_memory_space_constraint(layer_factor.T, pltpu.HBM)

    send1, keep1, ahead, factor = contract(lf, weights, col_factor)
    recv1 = shift(send1, "core", 2, 1)
    send2, keep2 = contract_last(lf, ahead, factor)
    recv2 = shift(send2, "core", 2, 1)
    v2a, v2b, v1a, v1b, v3a, v3b, ct = cross_part(keep1, recv1, row_factor, 0, 3, None)
    p1 = shift(v2a, "z", 4, 1)
    p2 = shift(v2b, "z", 4, 3)
    p3 = shift(v1b, "z", 4, 1)
    p4 = shift(v3a, "z", 4, 3)
    v0a, v0b, ct = cross_part(keep2, recv2, row_factor, 3, 1, ct)
    cross = sum_over_planes(ct)
    rows = BLOCK // 2
    s1, s3 = call(relay_kernel, [shape(rows, HALF)] * 2, [v1a, p1, v3b, p2])
    p5 = shift(s1, "z", 4, 1)
    p6 = shift(s3, "z", 4, 3)

    away, ka = call(block_kernel, [shape(rows, HALF)] * 2, [v0a, p5, p4, v0b, p3, p6])
    kb = shift(away, "yhi", 2, 1)

    zp, u = call(
        rows_kernel,
        [shape(rows, RC), shape(rows, HALF)],
        [cross, ka, kb],
        scratch=[pltpu.VMEM((RC, HALF), f32)],
    )
    zr = shift(zp, "core", 2, 1)
    z, ct = call(core_kernel, [shape(rows // 2, RC), shape(*ct.shape)], [zp, zr, u])

    zy = shift(z, "yhi", 2, 1)
    both = call(join_kernel, shape(rows, RC), [z, zy])
    gathered = [both] + [shift(both, "z", 4, k) for k in (1, 2, 3)]
    four = call(join_kernel, shape(4 * rows, RC), gathered)
    other = shift(four, "core", 2, 1)
    row_update = call(finish_rows_kernel, shape(8 * rows, RC), [four, other])

    mine = sum_over_chips(ct)
    other = shift(mine, "core", 2, 1)
    core_out = call(finish_core_kernel, shape(RC, 2 * HALF), [mine, other])
    return row_update, core_out


def solution(mesh):
    fine = Mesh(mesh.devices.reshape(2, 2, 4, 4, 2), AXES)
    return jax.shard_map(
        body,
        mesh=fine,
        in_specs=(
            P("yhi", ("ylo", "x"), ("z", "core")),
            P(("z", "core"), None),
            P("yhi", None),
            P(("ylo", "x"), None),
        ),
        out_specs=(P(("ylo", "x"), None), P()),
        check_vma=False,
    )
```

```python
import functools

import jax
import jax.numpy as jnp
from jax import lax
from jax.experimental import pallas as pl
from jax.experimental.pallas import tpu as pltpu
from jax.sharding import Mesh, PartitionSpec as P


R = 8192
RC = 256
RL = 4

AXES = ("yhi", "ylo", "x", "z", "core")
PLANE = AXES[:3]
CHIPS = AXES[:4]
SUB = 64
BLOCK = 256
HALF = RL * RC // 2
COLS = HALF // 128
f32 = jnp.float32
bf16 = jnp.bfloat16
SMEM = pl.BlockSpec(memory_space=pltpu.SMEM)
VMEM = pl.BlockSpec(memory_space=pltpu.VMEM)
MIB = 1 << 20


def parts_of(v):
    hi = v.astype(bf16)
    return hi, (v - hi.astype(f32)).astype(bf16)


def dot3(a, b, dims):
    ah, al = parts_of(a)
    bh, bl = parts_of(b)

    def dot(p, q):
        return lax.dot_general(p, q, (dims, ((), ())), preferred_element_type=f32)

    return dot(ah, bh) + (dot(ah, bl) + dot(al, bh))


def call(kernel, outs, ops, smem=0, scratch=(), vmem=16, cost=None):
    return pl.pallas_call(
        kernel,
        out_shape=outs,
        in_specs=[SMEM] * smem + [VMEM] * (len(ops) - smem),
        out_specs=jax.tree.map(lambda _: VMEM, outs),
        scratch_shapes=list(scratch),
        compiler_params=pltpu.CompilerParams(vmem_limit_bytes=vmem * MIB),
        cost_estimate=cost,
    )(*ops)


def shape(*dims):
    return jax.ShapeDtypeStruct(dims, f32)


def half_block(i):
    away = (2, 1, 3, 0)[i // 2]
    return ((lax.axis_index("z") + away) % 4) * 2 + (lax.axis_index("yhi") + 1 - i % 2) % 2


def mix_columns(lf, d, subs, send, keep):
    layers = d.shape[1]
    theirs = (1 - lax.axis_index("core")) * (RL // 2)
    step = 16
    for s in subs:
        for r in range(0, SUB, step):
            v = [d[s, l, r : r + step, :] for l in range(layers)]
            for base, out in ((theirs, send), (RL // 2 - theirs, keep)):
                for j in range(RL // 2):
                    acc = v[0] * lf[base + j, 0]
                    for l in range(1, layers):
                        acc = acc + v[l] * lf[base + j, l]
                    out[s * SUB + r : s * SUB + r + step, j * RC : (j + 1) * RC] = acc


def contract_kernel(lf, w, c, send, keep, ahead, c_copy, wbuf, d, sems):
    layers, _, cols = w.shape
    count, last = wbuf.shape[0], ahead.shape[0]
    per = BLOCK // 2 // SUB

    def copy(s):
        row = half_block(s // per) * (BLOCK // 2) + s % per * SUB
        rows = pl.ds(pl.multiple_of(row, SUB), SUB)
        target = wbuf.at[s] if s < count else ahead.at[s - count]
        return pltpu.make_async_copy(w.at[:, rows, :], target, sems.at[s])

    fetch = pltpu.make_async_copy(c, c_copy, sems.at[count + last])
    fetch.start()
    for s in range(count + last):
        copy(s).start()
    fetch.wait()
    at = 0
    for size in (1, 3) + (4,) * (count // 4 - 1):
        subs = range(at, at + size)
        for s in subs:
            copy(s).wait()
        for s in subs:
            part = wbuf[s].reshape(layers * SUB, cols)
            d[s] = jnp.dot(part, c_copy[...], preferred_element_type=f32).reshape(layers, SUB, RC)
        mix_columns(lf, d, subs, send, keep)
        at += size
    for s in range(count, count + last):
        copy(s).wait()


def contract(lf, w, c):
    layers, rows, cols = w.shape
    count = (rows - BLOCK) // SUB
    last = BLOCK // SUB
    out = shape(rows - BLOCK, HALF)
    hbm = pl.BlockSpec(memory_space=pl.ANY)
    return pl.pallas_call(
        contract_kernel,
        out_shape=(
            out,
            out,
            jax.ShapeDtypeStruct((last, layers, SUB, cols), bf16),
            jax.ShapeDtypeStruct(c.shape, bf16),
        ),
        in_specs=[SMEM, hbm, hbm],
        out_specs=(VMEM,) * 4,
        scratch_shapes=[
            pltpu.VMEM((count, layers, SUB, cols), bf16),
            pltpu.VMEM((count, layers, SUB, RC), f32),
            pltpu.SemaphoreType.DMA((count + last + 1,)),
        ],
        compiler_params=pltpu.CompilerParams(vmem_limit_bytes=40 * MIB),
        cost_estimate=pl.CostEstimate(
            flops=2 * layers * (rows - BLOCK) * cols * RC,
            bytes_accessed=2 * layers * rows * cols,
            transcendentals=0,
        ),
        name="contract",
    )(lf, w, c)


def contract_last_kernel(lf, w, c, send, keep, d):
    last, layers, _, cols = w.shape
    for s in range(last):
        part = w[s].reshape(layers * SUB, cols)
        d[s] = jnp.dot(part, c[...], preferred_element_type=f32).reshape(layers, SUB, RC)
    mix_columns(lf, d, range(last), send, keep)


def contract_last(lf, w, c):
    last, layers, _, cols = w.shape
    return call(
        contract_last_kernel,
        [shape(BLOCK, HALF)] * 2,
        [lf, w, c],
        smem=1,
        scratch=[pltpu.VMEM((last, layers, SUB, RC), f32)],
        cost=pl.CostEstimate(
            flops=2 * layers * BLOCK * cols * RC, bytes_accessed=MIB, transcendentals=0
        ),
    )


def cross_kernel(first, places, keep, recv, rf, *refs):
    blocks = len({place[0] for place in places})
    prior = refs[0] if len(refs) > blocks + 1 else None
    outs, ct = refs[-blocks - 1 : -1], refs[-1]
    half = BLOCK // 2
    total = None
    for n in range(len(places) // 2):
        v = keep[n * BLOCK : (n + 1) * BLOCK] + recv[n * BLOCK : (n + 1) * BLOCK]
        for h, (i, at) in enumerate(places[2 * n : 2 * n + 2]):
            outs[i][at * half : (at + 1) * half] = v[h * half : (h + 1) * half]
        f = jnp.concatenate(
            [
                rf[pl.ds(pl.multiple_of(half_block(2 * (first + n) + h) * half, half), half), :]
                for h in range(2)
            ],
            axis=0,
        )
        term = dot3(f, v, ((0,), (0,)))
        total = term if total is None else total + term
    for a in range(RC // 8):
        for b in range(COLS):
            t = total[8 * a : 8 * a + 8, 128 * b : 128 * b + 128]
            if prior is not None:
                t = t + prior[a * COLS + b]
            ct[a * COLS + b] = t


def cross_part(keep, recv, rf, first, places, prior):
    ops = [keep, recv, rf] + ([] if prior is None else [prior])
    sizes = [sum(p[0] == i for p in places) for i in range(len({p[0] for p in places}))]
    return call(
        functools.partial(cross_kernel, first, places),
        [shape(n * BLOCK // 2, HALF) for n in sizes] + [shape(RC * HALF // 1024, 8, 128)],
        ops,
        vmem=20,
        cost=pl.CostEstimate(
            flops=3 * len(places) * BLOCK * RC * HALF, bytes_accessed=4 * MIB, transcendentals=0
        ),
    )


def rows_kernel(ct, ka, kb, zp, u, full):
    for a in range(RC // 8):
        for b in range(COLS):
            full[8 * a : 8 * a + 8, 128 * b : 128 * b + 128] = ct[a * COLS + b]
    v = ka[...] + kb[...]
    u[...] = v
    zp[...] = dot3(v, full[...], ((1,), (1,)))


def core_kernel(zp, zr, u, z, ct):
    width_scale = 1.0 / jnp.sqrt(f32(RL * RC))
    row_scale = 1.0 / jnp.sqrt(f32(R))
    rows = (zp[...] + zr[...]) * width_scale
    half = rows.shape[0] // 2
    mine = pl.ds(pl.multiple_of(lax.axis_index("core") * half, half), half)
    z[...] = (zp[mine] + zr[mine]) * width_scale
    core = dot3(rows, u[...], ((0,), (0,))) * row_scale
    for a in range(RC // 8):
        for b in range(COLS):
            ct[a * COLS + b] = core[8 * a : 8 * a + 8, 128 * b : 128 * b + 128]


def finish_core_kernel(mine, other, out):
    core = lax.axis_index("core")
    for ref, at in ((mine, core), (other, 1 - core)):
        for b in range(COLS):
            lane = pl.ds(pl.multiple_of(at * HALF + 128 * b, 128), 128)
            for a in range(RC // 8):
                out[8 * a : 8 * a + 8, lane] = ref[a * COLS + b]


def finish_rows_kernel(mine, other, out):
    z, yhi, core = (lax.axis_index(a) for a in ("z", "yhi", "core"))
    quarter = BLOCK // 4
    for ref, at in ((mine, core), (other, 1 - core)):
        for k in range(4):
            base = ((z + 4 - k) % 4) * BLOCK + at * quarter
            for n in range(2):
                row = base + (yhi + n) % 2 * (BLOCK // 2)
                rows = pl.ds(pl.multiple_of(row, quarter), quarter)
                i = (2 * k + n) * quarter
                out[rows, :] = ref[i : i + quarter, :]


def relay_kernel(a, b, below, above, ab, cd):
    half = BLOCK // 2
    ab[...] = a[...] + below[:half]
    cd[...] = b[...] + above[:half]


def block_kernel(a, b, below, above, a2, b2, away, keep):
    half = BLOCK // 2
    away[...] = (a[...] + a2[...]) + above[half:]
    keep[...] = (b[...] + b2[...]) + below[half:]


def gathered_kernel(v, out):
    total = v[0]
    for i in range(1, v.shape[0]):
        total = total + v[i]
    out[...] = total


def spread_kernel(*refs):
    out = refs[-1]
    if len(refs) == 2:
        v = refs[0][0]
        for i in range(1, out.shape[0]):
            v = v + refs[0][i]
    else:
        s, s1, s2, s3 = (ref[...] for ref in refs[:-1])
        v = (s + s2) + (s1 + s3)
    for i in range(out.shape[0]):
        out[i] = v


def join_kernel(*refs):
    out = refs[-1]
    rows = refs[0].shape[0]
    for i, ref in enumerate(refs[:-1]):
        out[i * rows : (i + 1) * rows] = ref[...]


def shift(v, axis, size, by):
    return lax.ppermute(v, axis, [(i, (i + by) % size) for i in range(size)])


def exchange(v, axes):
    return lax.all_to_all(v, axes, 0, 0, tiled=True)


def sum_over_planes(tiles):
    n = lax.axis_size(PLANE)
    v = exchange(tiles.reshape(n, -1, 128), PLANE)
    s = call(gathered_kernel, shape(*v.shape[1:]), [v])
    s1, s2, s3 = (shift(s, "z", 4, k) for k in (1, 2, 3))
    b = call(spread_kernel, shape(*v.shape), [s, s1, s2, s3])
    return exchange(b, PLANE).reshape(tiles.shape)


def sum_over_chips(tiles):
    n = lax.axis_size(CHIPS)
    v = exchange(tiles.reshape(n, -1, 128), CHIPS)
    b = call(spread_kernel, shape(*v.shape), [v])
    return exchange(b, CHIPS).reshape(tiles.shape)


def body(weights, col_factor, layer_factor, row_factor):
    weights, col_factor = (pltpu.with_memory_space_constraint(v, pltpu.HBM) for v in (weights, col_factor))
    lf = pltpu.with_memory_space_constraint(layer_factor.T, pltpu.HBM)

    send1, keep1, ahead, factor = contract(lf, weights, col_factor)
    recv1 = shift(send1, "core", 2, 1)
    send2, keep2 = contract_last(lf, ahead, factor)
    recv2 = shift(send2, "core", 2, 1)
    up, down, v1a, v3b, ct = cross_part(
        keep1, recv1, row_factor, 0, ((0, 0), (1, 0), (2, 0), (0, 1), (1, 1), (3, 0)), None
    )
    p1 = shift(up, "z", 4, 1)
    p2 = shift(down, "z", 4, 3)
    v0a, v0b, ct = cross_part(keep2, recv2, row_factor, 3, ((0, 0), (1, 0)), ct)
    cross = sum_over_planes(ct)
    rows = BLOCK // 2
    s1, s3 = call(relay_kernel, [shape(rows, HALF)] * 2, [v1a, v3b, p1, p2])
    p5 = shift(s1, "z", 4, 1)
    p6 = shift(s3, "z", 4, 3)

    away, ka = call(block_kernel, [shape(rows, HALF)] * 2, [v0a, v0b, p1, p2, p5, p6])
    kb = shift(away, "yhi", 2, 1)

    zp, u = call(
        rows_kernel,
        [shape(rows, RC), shape(rows, HALF)],
        [cross, ka, kb],
        scratch=[pltpu.VMEM((RC, HALF), f32)],
    )
    zr = shift(zp, "core", 2, 1)
    z, ct = call(core_kernel, [shape(rows // 2, RC), shape(*ct.shape)], [zp, zr, u])

    zy = shift(z, "yhi", 2, 1)
    both = call(join_kernel, shape(rows, RC), [z, zy])
    gathered = [both] + [shift(both, "z", 4, k) for k in (1, 2, 3)]
    four = call(join_kernel, shape(4 * rows, RC), gathered)
    other = shift(four, "core", 2, 1)
    row_update = call(finish_rows_kernel, shape(8 * rows, RC), [four, other])

    mine = sum_over_chips(ct)
    other = shift(mine, "core", 2, 1)
    core_out = call(finish_core_kernel, shape(RC, 2 * HALF), [mine, other])
    return row_update, core_out


def solution(mesh):
    fine = Mesh(mesh.devices.reshape(2, 2, 4, 4, 2), AXES)
    return jax.shard_map(
        body,
        mesh=fine,
        in_specs=(
            P("yhi", ("ylo", "x"), ("z", "core")),
            P(("z", "core"), None),
            P("yhi", None),
            P(("ylo", "x"), None),
        ),
        out_specs=(P(("ylo", "x"), None), P()),
        check_vma=False,
    )
```

```python
import functools

import jax
import jax.numpy as jnp
from jax import lax
from jax.experimental import pallas as pl
from jax.experimental.pallas import tpu as pltpu
from jax.sharding import Mesh, PartitionSpec as P


R = 8192
RC = 256
RL = 4

AXES = ("yhi", "ylo", "x", "z", "core")
PLANE = AXES[:3]
SUB = 64
BLOCK = 256
HALF = RL * RC // 2
COLS = HALF // 128
f32 = jnp.float32
bf16 = jnp.bfloat16
SMEM = pl.BlockSpec(memory_space=pltpu.SMEM)
VMEM = pl.BlockSpec(memory_space=pltpu.VMEM)
MIB = 1 << 20


def parts_of(v):
    hi = v.astype(bf16)
    return hi, (v - hi.astype(f32)).astype(bf16)


def dot3(a, b, dims):
    ah, al = parts_of(a)
    bh, bl = parts_of(b)

    def dot(p, q):
        return lax.dot_general(p, q, (dims, ((), ())), preferred_element_type=f32)

    return dot(ah, bh) + (dot(ah, bl) + dot(al, bh))


def call(kernel, outs, ops, smem=0, scratch=(), vmem=16, cost=None):
    return pl.pallas_call(
        kernel,
        out_shape=outs,
        in_specs=[SMEM] * smem + [VMEM] * (len(ops) - smem),
        out_specs=jax.tree.map(lambda _: VMEM, outs),
        scratch_shapes=list(scratch),
        compiler_params=pltpu.CompilerParams(vmem_limit_bytes=vmem * MIB),
        cost_estimate=cost,
    )(*ops)


def shape(*dims):
    return jax.ShapeDtypeStruct(dims, f32)


def half_block(i):
    away = (2, 1, 3, 0)[i // 2]
    return ((lax.axis_index("z") + away) % 4) * 2 + (lax.axis_index("yhi") + 1 - i % 2) % 2


def mix_columns(lf, d, subs, send, keep):
    layers = d.shape[1]
    theirs = (1 - lax.axis_index("core")) * (RL // 2)
    step = 16
    for s in subs:
        for r in range(0, SUB, step):
            v = [d[s, l, r : r + step, :] for l in range(layers)]
            for base, out in ((theirs, send), (RL // 2 - theirs, keep)):
                for j in range(RL // 2):
                    acc = v[0] * lf[base + j, 0]
                    for l in range(1, layers):
                        acc = acc + v[l] * lf[base + j, l]
                    out[s * SUB + r : s * SUB + r + step, j * RC : (j + 1) * RC] = acc


def contract_kernel(lf, w, c, send, keep, ahead, c_copy, wbuf, d, sems):
    layers, _, cols = w.shape
    count, last = wbuf.shape[0], ahead.shape[0]
    per = BLOCK // 2 // SUB

    def copy(s):
        row = half_block(s // per) * (BLOCK // 2) + s % per * SUB
        rows = pl.ds(pl.multiple_of(row, SUB), SUB)
        target = wbuf.at[s] if s < count else ahead.at[s - count]
        return pltpu.make_async_copy(w.at[:, rows, :], target, sems.at[s])

    fetch = pltpu.make_async_copy(c, c_copy, sems.at[count + last])
    fetch.start()
    for s in range(count + last):
        copy(s).start()
    fetch.wait()
    at = 0
    for size in (1, 3) + (4,) * (count // 4 - 1):
        subs = range(at, at + size)
        for s in subs:
            copy(s).wait()
        for s in subs:
            part = wbuf[s].reshape(layers * SUB, cols)
            d[s] = jnp.dot(part, c_copy[...], preferred_element_type=f32).reshape(layers, SUB, RC)
        mix_columns(lf, d, subs, send, keep)
        at += size
    for s in range(count, count + last):
        copy(s).wait()


def contract(lf, w, c):
    layers, rows, cols = w.shape
    count = (rows - BLOCK) // SUB
    last = BLOCK // SUB
    out = shape(rows - BLOCK, HALF)
    hbm = pl.BlockSpec(memory_space=pl.ANY)
    return pl.pallas_call(
        contract_kernel,
        out_shape=(
            out,
            out,
            jax.ShapeDtypeStruct((last, layers, SUB, cols), bf16),
            jax.ShapeDtypeStruct(c.shape, bf16),
        ),
        in_specs=[SMEM, hbm, hbm],
        out_specs=(VMEM,) * 4,
        scratch_shapes=[
            pltpu.VMEM((count, layers, SUB, cols), bf16),
            pltpu.VMEM((count, layers, SUB, RC), f32),
            pltpu.SemaphoreType.DMA((count + last + 1,)),
        ],
        compiler_params=pltpu.CompilerParams(vmem_limit_bytes=40 * MIB),
        cost_estimate=pl.CostEstimate(
            flops=2 * layers * (rows - BLOCK) * cols * RC,
            bytes_accessed=2 * layers * rows * cols,
            transcendentals=0,
        ),
        name="contract",
    )(lf, w, c)


def contract_last_kernel(lf, w, c, send, keep, d):
    last, layers, _, cols = w.shape
    for s in range(last):
        part = w[s].reshape(layers * SUB, cols)
        d[s] = jnp.dot(part, c[...], preferred_element_type=f32).reshape(layers, SUB, RC)
    mix_columns(lf, d, range(last), send, keep)


def contract_last(lf, w, c):
    last, layers, _, cols = w.shape
    return call(
        contract_last_kernel,
        [shape(BLOCK, HALF)] * 2,
        [lf, w, c],
        smem=1,
        scratch=[pltpu.VMEM((last, layers, SUB, RC), f32)],
        cost=pl.CostEstimate(
            flops=2 * layers * BLOCK * cols * RC, bytes_accessed=MIB, transcendentals=0
        ),
    )


def cross_kernel(first, places, keep, recv, rf, *refs):
    blocks = len({place[0] for place in places})
    prior = refs[0] if len(refs) > blocks + 1 else None
    outs, ct = refs[-blocks - 1 : -1], refs[-1]
    half = BLOCK // 2
    total = None
    for n in range(len(places) // 2):
        v = keep[n * BLOCK : (n + 1) * BLOCK] + recv[n * BLOCK : (n + 1) * BLOCK]
        for h, (i, at) in enumerate(places[2 * n : 2 * n + 2]):
            outs[i][at * half : (at + 1) * half] = v[h * half : (h + 1) * half]
        f = jnp.concatenate(
            [
                rf[pl.ds(pl.multiple_of(half_block(2 * (first + n) + h) * half, half), half), :]
                for h in range(2)
            ],
            axis=0,
        )
        term = dot3(f, v, ((0,), (0,)))
        total = term if total is None else total + term
    for a in range(RC // 8):
        for b in range(COLS):
            t = total[8 * a : 8 * a + 8, 128 * b : 128 * b + 128]
            if prior is not None:
                t = t + prior[a * COLS + b]
            ct[a * COLS + b] = t


def cross_part(keep, recv, rf, first, places, prior):
    ops = [keep, recv, rf] + ([] if prior is None else [prior])
    sizes = [sum(p[0] == i for p in places) for i in range(len({p[0] for p in places}))]
    return call(
        functools.partial(cross_kernel, first, places),
        [shape(n * BLOCK // 2, HALF) for n in sizes] + [shape(RC * HALF // 1024, 8, 128)],
        ops,
        vmem=20,
        cost=pl.CostEstimate(
            flops=3 * len(places) * BLOCK * RC * HALF, bytes_accessed=4 * MIB, transcendentals=0
        ),
    )


def rows_kernel(ct, ka, kb, zp, u, full):
    for a in range(RC // 8):
        for b in range(COLS):
            full[8 * a : 8 * a + 8, 128 * b : 128 * b + 128] = ct[a * COLS + b]
    v = ka[...] + kb[...]
    u[...] = v
    zp[...] = dot3(v, full[...], ((1,), (1,)))


def core_kernel(zp, zr, u, z, ct):
    width_scale = 1.0 / jnp.sqrt(f32(RL * RC))
    row_scale = 1.0 / jnp.sqrt(f32(R))
    rows = (zp[...] + zr[...]) * width_scale
    half = rows.shape[0] // 2
    mine = pl.ds(pl.multiple_of(lax.axis_index("core") * half, half), half)
    z[...] = (zp[mine] + zr[mine]) * width_scale
    core = dot3(rows, u[...], ((0,), (0,))) * row_scale
    for a in range(RC // 8):
        for b in range(COLS):
            ct[a * COLS + b] = core[8 * a : 8 * a + 8, 128 * b : 128 * b + 128]


def finish_core_kernel(mine, other, out):
    core = lax.axis_index("core")
    for ref, at in ((mine, core), (other, 1 - core)):
        for b in range(COLS):
            lane = pl.ds(pl.multiple_of(at * HALF + 128 * b, 128), 128)
            for a in range(RC // 8):
                out[8 * a : 8 * a + 8, lane] = ref[a * COLS + b]


def finish_rows_kernel(mine, other, out):
    z, yhi, core = (lax.axis_index(a) for a in ("z", "yhi", "core"))
    quarter = BLOCK // 4
    for ref, at in ((mine, core), (other, 1 - core)):
        for k in range(4):
            base = ((z + 4 - k) % 4) * BLOCK + at * quarter
            for n in range(2):
                row = base + (yhi + n) % 2 * (BLOCK // 2)
                rows = pl.ds(pl.multiple_of(row, quarter), quarter)
                i = (2 * k + n) * quarter
                out[rows, :] = ref[i : i + quarter, :]


def relay_kernel(a, b, below, above, ab, cd):
    half = BLOCK // 2
    ab[...] = a[...] + below[:half]
    cd[...] = b[...] + above[:half]


def block_kernel(a, b, below, above, a2, b2, away, keep):
    half = BLOCK // 2
    away[...] = (a[...] + a2[...]) + above[half:]
    keep[...] = (b[...] + b2[...]) + below[half:]


def gathered_kernel(v, out):
    total = v[0]
    for i in range(1, v.shape[0]):
        total = total + v[i]
    out[...] = total


def spread_kernel(*refs):
    out = refs[-1]
    if len(refs) == 2:
        v = refs[0][0]
        for i in range(1, out.shape[0]):
            v = v + refs[0][i]
    else:
        s, s1, s2, s3 = (ref[...] for ref in refs[:-1])
        v = (s + s2) + (s1 + s3)
    for i in range(out.shape[0]):
        out[i] = v


def join_kernel(*refs):
    out = refs[-1]
    rows = refs[0].shape[0]
    for i, ref in enumerate(refs[:-1]):
        out[i * rows : (i + 1) * rows] = ref[...]


def shift(v, axis, size, by):
    return lax.ppermute(v, axis, [(i, (i + by) % size) for i in range(size)])


def exchange(v, axes):
    return lax.all_to_all(v, axes, 0, 0, tiled=True)


def sum_over_planes(tiles):
    n = lax.axis_size(PLANE)
    v = exchange(tiles.reshape(n, -1, 128), PLANE)
    s = call(gathered_kernel, shape(*v.shape[1:]), [v])
    s1, s2, s3 = (shift(s, "z", 4, k) for k in (1, 2, 3))
    b = call(spread_kernel, shape(*v.shape), [s, s1, s2, s3])
    return exchange(b, PLANE).reshape(tiles.shape)


def body(weights, col_factor, layer_factor, row_factor):
    weights, col_factor = (pltpu.with_memory_space_constraint(v, pltpu.HBM) for v in (weights, col_factor))
    lf = pltpu.with_memory_space_constraint(layer_factor.T, pltpu.HBM)

    send1, keep1, ahead, factor = contract(lf, weights, col_factor)
    recv1 = shift(send1, "core", 2, 1)
    send2, keep2 = contract_last(lf, ahead, factor)
    recv2 = shift(send2, "core", 2, 1)
    up, down, v1a, v3b, ct = cross_part(
        keep1, recv1, row_factor, 0, ((0, 0), (1, 0), (2, 0), (0, 1), (1, 1), (3, 0)), None
    )
    p1 = shift(up, "z", 4, 1)
    p2 = shift(down, "z", 4, 3)
    v0a, v0b, ct = cross_part(keep2, recv2, row_factor, 3, ((0, 0), (1, 0)), ct)
    cross = sum_over_planes(ct)
    rows = BLOCK // 2
    s1, s3 = call(relay_kernel, [shape(rows, HALF)] * 2, [v1a, v3b, p1, p2])
    p5 = shift(s1, "z", 4, 1)
    p6 = shift(s3, "z", 4, 3)

    away, ka = call(block_kernel, [shape(rows, HALF)] * 2, [v0a, v0b, p1, p2, p5, p6])
    kb = shift(away, "yhi", 2, 1)

    zp, u = call(
        rows_kernel,
        [shape(rows, RC), shape(rows, HALF)],
        [cross, ka, kb],
        scratch=[pltpu.VMEM((RC, HALF), f32)],
    )
    zr = shift(zp, "core", 2, 1)
    z, ct = call(core_kernel, [shape(rows // 2, RC), shape(*ct.shape)], [zp, zr, u])

    zy = shift(z, "yhi", 2, 1)
    both = call(join_kernel, shape(rows, RC), [z, zy])
    gathered = [both] + [shift(both, "z", 4, k) for k in (1, 2, 3)]
    four = call(join_kernel, shape(4 * rows, RC), gathered)
    other = shift(four, "core", 2, 1)
    row_update = call(finish_rows_kernel, shape(8 * rows, RC), [four, other])

    mine = sum_over_planes(ct)
    other = shift(mine, "core", 2, 1)
    core_out = call(finish_core_kernel, shape(RC, 2 * HALF), [mine, other])
    return row_update, core_out


def solution(mesh):
    fine = Mesh(mesh.devices.reshape(2, 2, 4, 4, 2), AXES)
    return jax.shard_map(
        body,
        mesh=fine,
        in_specs=(
            P("yhi", ("ylo", "x"), ("z", "core")),
            P(("z", "core"), None),
            P("yhi", None),
            P(("ylo", "x"), None),
        ),
        out_specs=(P(("ylo", "x"), None), P()),
        check_vma=False,
    )
```

```python
import functools

import jax
import jax.numpy as jnp
from jax import lax
from jax.experimental import pallas as pl
from jax.experimental.pallas import tpu as pltpu
from jax.sharding import Mesh, PartitionSpec as P


R = 8192
RC = 256
RL = 4

AXES = ("yhi", "ylo", "x", "z", "core")
PLANE = AXES[:3]
SUB = 64
BLOCK = 256
HALF = RL * RC // 2
COLS = HALF // 128
f32 = jnp.float32
bf16 = jnp.bfloat16
SMEM = pl.BlockSpec(memory_space=pltpu.SMEM)
VMEM = pl.BlockSpec(memory_space=pltpu.VMEM)
MIB = 1 << 20


def parts_of(v):
    hi = v.astype(bf16)
    return hi, (v - hi.astype(f32)).astype(bf16)


def dot3(a, b, dims):
    ah, al = parts_of(a)
    bh, bl = parts_of(b)

    def dot(p, q):
        return lax.dot_general(p, q, (dims, ((), ())), preferred_element_type=f32)

    return dot(ah, bh) + (dot(ah, bl) + dot(al, bh))


def call(kernel, outs, ops, smem=0, scratch=(), vmem=16, cost=None):
    return pl.pallas_call(
        kernel,
        out_shape=outs,
        in_specs=[SMEM] * smem + [VMEM] * (len(ops) - smem),
        out_specs=jax.tree.map(lambda _: VMEM, outs),
        scratch_shapes=list(scratch),
        compiler_params=pltpu.CompilerParams(vmem_limit_bytes=vmem * MIB),
        cost_estimate=cost,
    )(*ops)


def shape(*dims):
    return jax.ShapeDtypeStruct(dims, f32)


def half_block(i):
    away = (2, 1, 3, 0)[i // 2]
    return ((lax.axis_index("z") + away) % 4) * 2 + (lax.axis_index("yhi") + 1 - i % 2) % 2


def mix_columns(lf, d, subs, send, keep):
    layers = d.shape[1]
    theirs = (1 - lax.axis_index("core")) * (RL // 2)
    step = 16
    for s in subs:
        for r in range(0, SUB, step):
            v = [d[s, l, r : r + step, :] for l in range(layers)]
            for base, out in ((theirs, send), (RL // 2 - theirs, keep)):
                for j in range(RL // 2):
                    acc = v[0] * lf[base + j, 0]
                    for l in range(1, layers):
                        acc = acc + v[l] * lf[base + j, l]
                    out[s * SUB + r : s * SUB + r + step, j * RC : (j + 1) * RC] = acc


def contract_kernel(lf, w, c, send, keep, ahead, c_copy, wbuf, d, sems):
    layers, _, cols = w.shape
    count, last = wbuf.shape[0], ahead.shape[0]
    per = BLOCK // 2 // SUB

    def copy(s):
        row = half_block(s // per) * (BLOCK // 2) + s % per * SUB
        rows = pl.ds(pl.multiple_of(row, SUB), SUB)
        target = wbuf.at[s] if s < count else ahead.at[s - count]
        return pltpu.make_async_copy(w.at[:, rows, :], target, sems.at[s])

    fetch = pltpu.make_async_copy(c, c_copy, sems.at[count + last])
    fetch.start()
    for s in range(count + last):
        copy(s).start()
    fetch.wait()
    at = 0
    for size in (1, 3) + (4,) * (count // 4 - 1):
        subs = range(at, at + size)
        for s in subs:
            copy(s).wait()
        for s in subs:
            part = wbuf[s].reshape(layers * SUB, cols)
            d[s] = jnp.dot(part, c_copy[...], preferred_element_type=f32).reshape(layers, SUB, RC)
        mix_columns(lf, d, subs, send, keep)
        at += size
    for s in range(count, count + last):
        copy(s).wait()


def contract(lf, w, c):
    layers, rows, cols = w.shape
    count = (rows - BLOCK) // SUB
    last = BLOCK // SUB
    out = shape(rows - BLOCK, HALF)
    hbm = pl.BlockSpec(memory_space=pl.ANY)
    return pl.pallas_call(
        contract_kernel,
        out_shape=(
            out,
            out,
            jax.ShapeDtypeStruct((last, layers, SUB, cols), bf16),
            jax.ShapeDtypeStruct(c.shape, bf16),
        ),
        in_specs=[SMEM, hbm, hbm],
        out_specs=(VMEM,) * 4,
        scratch_shapes=[
            pltpu.VMEM((count, layers, SUB, cols), bf16),
            pltpu.VMEM((count, layers, SUB, RC), f32),
            pltpu.SemaphoreType.DMA((count + last + 1,)),
        ],
        compiler_params=pltpu.CompilerParams(vmem_limit_bytes=40 * MIB),
        cost_estimate=pl.CostEstimate(
            flops=2 * layers * (rows - BLOCK) * cols * RC,
            bytes_accessed=2 * layers * rows * cols,
            transcendentals=0,
        ),
        name="contract",
    )(lf, w, c)


def contract_last_kernel(lf, w, c, send, keep, d):
    last, layers, _, cols = w.shape
    for s in range(last):
        part = w[s].reshape(layers * SUB, cols)
        d[s] = jnp.dot(part, c[...], preferred_element_type=f32).reshape(layers, SUB, RC)
    mix_columns(lf, d, range(last), send, keep)


def contract_last(lf, w, c):
    last, layers, _, cols = w.shape
    return call(
        contract_last_kernel,
        [shape(BLOCK, HALF)] * 2,
        [lf, w, c],
        smem=1,
        scratch=[pltpu.VMEM((last, layers, SUB, RC), f32)],
        cost=pl.CostEstimate(
            flops=2 * layers * BLOCK * cols * RC, bytes_accessed=MIB, transcendentals=0
        ),
    )


def cross_kernel(first, places, keep, recv, rf, *refs):
    blocks = len({place[0] for place in places})
    prior = refs[0] if len(refs) > blocks + 1 else None
    outs, ct = refs[-blocks - 1 : -1], refs[-1]
    half = BLOCK // 2
    total = None
    for n in range(len(places) // 2):
        v = keep[n * BLOCK : (n + 1) * BLOCK] + recv[n * BLOCK : (n + 1) * BLOCK]
        for h, (i, at) in enumerate(places[2 * n : 2 * n + 2]):
            outs[i][at * half : (at + 1) * half] = v[h * half : (h + 1) * half]
        f = jnp.concatenate(
            [
                rf[pl.ds(pl.multiple_of(half_block(2 * (first + n) + h) * half, half), half), :]
                for h in range(2)
            ],
            axis=0,
        )
        term = dot3(f, v, ((0,), (0,)))
        total = term if total is None else total + term
    for a in range(RC // 8):
        for b in range(COLS):
            t = total[8 * a : 8 * a + 8, 128 * b : 128 * b + 128]
            if prior is not None:
                t = t + prior[a * COLS + b]
            ct[a * COLS + b] = t


def cross_part(keep, recv, rf, first, places, prior):
    ops = [keep, recv, rf] + ([] if prior is None else [prior])
    sizes = [sum(p[0] == i for p in places) for i in range(len({p[0] for p in places}))]
    return call(
        functools.partial(cross_kernel, first, places),
        [shape(n * BLOCK // 2, HALF) for n in sizes] + [shape(RC * HALF // 1024, 8, 128)],
        ops,
        vmem=20,
        cost=pl.CostEstimate(
            flops=3 * len(places) * BLOCK * RC * HALF, bytes_accessed=4 * MIB, transcendentals=0
        ),
    )


def rows_kernel(ct, ka, kb, zp, u, full):
    for a in range(RC // 8):
        for b in range(COLS):
            full[8 * a : 8 * a + 8, 128 * b : 128 * b + 128] = ct[a * COLS + b]
    v = ka[...] + kb[...]
    u[...] = v
    zp[...] = dot3(v, full[...], ((1,), (1,)))


def core_kernel(zp, zr, u, z, ct):
    width_scale = 1.0 / jnp.sqrt(f32(RL * RC))
    row_scale = 1.0 / jnp.sqrt(f32(R))
    rows = (zp[...] + zr[...]) * width_scale
    half = rows.shape[0] // 2
    mine = pl.ds(pl.multiple_of(lax.axis_index("core") * half, half), half)
    z[...] = (zp[mine] + zr[mine]) * width_scale
    core = dot3(rows, u[...], ((0,), (0,))) * row_scale
    for a in range(RC // 8):
        for b in range(COLS):
            ct[a * COLS + b] = core[8 * a : 8 * a + 8, 128 * b : 128 * b + 128]


def finish_core_kernel(mine, other, out):
    core = lax.axis_index("core")
    for ref, at in ((mine, core), (other, 1 - core)):
        for b in range(COLS):
            lane = pl.ds(pl.multiple_of(at * HALF + 128 * b, 128), 128)
            for a in range(RC // 8):
                out[8 * a : 8 * a + 8, lane] = ref[a * COLS + b]


def finish_rows_kernel(mine, other, out):
    z, yhi, core = (lax.axis_index(a) for a in ("z", "yhi", "core"))
    quarter = BLOCK // 4
    for ref, at in ((mine, core), (other, 1 - core)):
        for k in range(4):
            base = ((z + 4 - k) % 4) * BLOCK + at * quarter
            for n in range(2):
                row = base + (yhi + n) % 2 * (BLOCK // 2)
                rows = pl.ds(pl.multiple_of(row, quarter), quarter)
                i = (4 * n + k) * quarter
                out[rows, :] = ref[i : i + quarter, :]


def relay_kernel(a, b, below, above, ab, cd):
    half = BLOCK // 2
    ab[...] = a[...] + below[:half]
    cd[...] = b[...] + above[:half]


def block_kernel(a, b, below, above, a2, b2, away, keep):
    half = BLOCK // 2
    away[...] = (a[...] + a2[...]) + above[half:]
    keep[...] = (b[...] + b2[...]) + below[half:]


def gathered_kernel(v, out):
    total = v[0]
    for i in range(1, v.shape[0]):
        total = total + v[i]
    out[...] = total


def spread_kernel(*refs):
    out = refs[-1]
    if len(refs) == 2:
        v = refs[0][0]
        for i in range(1, out.shape[0]):
            v = v + refs[0][i]
    else:
        s, s1, s2, s3 = (ref[...] for ref in refs[:-1])
        v = (s + s2) + (s1 + s3)
    for i in range(out.shape[0]):
        out[i] = v


def join_kernel(*refs):
    out = refs[-1]
    rows = refs[0].shape[0]
    for i, ref in enumerate(refs[:-1]):
        out[i * rows : (i + 1) * rows] = ref[...]


def shift(v, axis, size, by):
    return lax.ppermute(v, axis, [(i, (i + by) % size) for i in range(size)])


def exchange(v, axes):
    return lax.all_to_all(v, axes, 0, 0, tiled=True)


def sum_over_planes(tiles):
    n = lax.axis_size(PLANE)
    v = exchange(tiles.reshape(n, -1, 128), PLANE)
    s = call(gathered_kernel, shape(*v.shape[1:]), [v])
    s1, s2, s3 = (shift(s, "z", 4, k) for k in (1, 2, 3))
    b = call(spread_kernel, shape(*v.shape), [s, s1, s2, s3])
    return exchange(b, PLANE).reshape(tiles.shape)


def body(weights, col_factor, layer_factor, row_factor):
    weights, col_factor = (pltpu.with_memory_space_constraint(v, pltpu.HBM) for v in (weights, col_factor))
    lf = pltpu.with_memory_space_constraint(layer_factor.T, pltpu.HBM)

    send1, keep1, ahead, factor = contract(lf, weights, col_factor)
    recv1 = shift(send1, "core", 2, 1)
    send2, keep2 = contract_last(lf, ahead, factor)
    recv2 = shift(send2, "core", 2, 1)
    up, down, v1a, v3b, ct = cross_part(
        keep1, recv1, row_factor, 0, ((0, 0), (1, 0), (2, 0), (0, 1), (1, 1), (3, 0)), None
    )
    p1 = shift(up, "z", 4, 1)
    p2 = shift(down, "z", 4, 3)
    v0a, v0b, ct = cross_part(keep2, recv2, row_factor, 3, ((0, 0), (1, 0)), ct)
    cross = sum_over_planes(ct)
    rows = BLOCK // 2
    s1, s3 = call(relay_kernel, [shape(rows, HALF)] * 2, [v1a, v3b, p1, p2])
    p5 = shift(s1, "z", 4, 1)
    p6 = shift(s3, "z", 4, 3)

    away, ka = call(block_kernel, [shape(rows, HALF)] * 2, [v0a, v0b, p1, p2, p5, p6])
    kb = shift(away, "yhi", 2, 1)

    zp, u = call(
        rows_kernel,
        [shape(rows, RC), shape(rows, HALF)],
        [cross, ka, kb],
        scratch=[pltpu.VMEM((RC, HALF), f32)],
    )
    zr = shift(zp, "core", 2, 1)
    z, ct = call(core_kernel, [shape(rows // 2, RC), shape(*ct.shape)], [zp, zr, u])

    gathered = [z] + [shift(z, "z", 4, k) for k in (1, 2, 3)]
    four = call(join_kernel, shape(2 * rows, RC), gathered)
    beyond = shift(four, "yhi", 2, 1)
    eight = call(join_kernel, shape(4 * rows, RC), [four, beyond])
    other = shift(eight, "core", 2, 1)
    row_update = call(finish_rows_kernel, shape(8 * rows, RC), [eight, other])

    mine = sum_over_planes(ct)
    other = shift(mine, "core", 2, 1)
    core_out = call(finish_core_kernel, shape(RC, 2 * HALF), [mine, other])
    return row_update, core_out


def solution(mesh):
    fine = Mesh(mesh.devices.reshape(2, 2, 4, 4, 2), AXES)
    return jax.shard_map(
        body,
        mesh=fine,
        in_specs=(
            P("yhi", ("ylo", "x"), ("z", "core")),
            P(("z", "core"), None),
            P("yhi", None),
            P(("ylo", "x"), None),
        ),
        out_specs=(P(("ylo", "x"), None), P()),
        check_vma=False,
    )
```
